128 devices in a mesh: split: 16 (over x, y_hi, core), shard: 8 (over y_lo, z).
Axes of the slice: x: 4, y: 4 (y_hi: 2, y_lo: 2; y = y_hi * 2 + y_lo), z: 4, core: 2. Of those that a mesh axis runs over, the one named last changes fastest.
Arguments:
- strain: bfloat16 [3, 4096], P(None, ('split', 'shard')), may hold values from -6 to 6
- basis: bfloat16 [16, 400, 2048], P('split', 'shard'), may hold values from -0.125 to 0.125
- recon: bfloat16 [16, 2, 4096, 400], P('split', None, 'shard'), may hold values from -0.3125 to 0.3125
Outputs:
- snr2: float32 [16, 4096, 2048], P('split', 'shard')
- loudest: float32 [2048], replicated
The draws below stay inside these ranges and needn't reach their ends.
All inputs are finite; a program needn't handle non-finite values.
Results may differ from the reference program's by a relative error of at most 0.0025.
Values may be sent and summed in bfloat16 or wider, within the bound.
No kernel may reach another device: no remote copies, remote signals or barrier semaphores. Data moves between devices by JAX's collectives and lax.ppermute only.
A program may use at most 128 MiB of HBM per device.

```python
import jax
import jax.numpy as jnp
from jax import lax

NDET = 3
NBASIS = 400
TAPS = 2048
TOUT = 2048
SAMPLES = 4096
NSPLIT = 16
TEMPLATES = 4096


def levels(stream_key, dims, cuts, low, top_value):
    factor_of, own = 1.0, jax.random.fold_in(stream_key, 6)
    for dim, shards_of in cuts:
        heights = jnp.exp(jax.random.uniform(jax.random.fold_in(own, dim), (shards_of,), jnp.float32, low / len(cuts), top_value / len(cuts)))
        factor_of = factor_of * jnp.repeat(heights, dims[dim] // shards_of).reshape([-1 if axis == dim else 1 for axis in range(len(dims))])
    return factor_of


def normal_values(rng, extent, deviation, most, cuts=(), kind=jnp.bfloat16):
    gain = levels(rng, extent, cuts, -0.22, 0.18) if cuts else 1.0
    values = jax.random.normal(rng, extent, jnp.float32) * deviation * gain
    return jnp.minimum(jnp.maximum(values, -most), most).astype(kind)


def setup_inputs(seed: int = 0) -> dict:
    streams_of = jax.random.split(jax.random.key(seed), 4)
    return {
        "strain": normal_values(streams_of[0], (NDET, SAMPLES), 1.0, 6.0, ((1, 128),)),
        "basis": normal_values(streams_of[1], (NSPLIT, NBASIS, TAPS), TAPS ** -0.5, 0.125, ((0, 16), (1, 8))),
        "recon": normal_values(streams_of[2], (NSPLIT, 2, TEMPLATES, NBASIS), NBASIS ** -0.5, 0.3125, ((0, 16), (2, 8))),
    }


def toeplitz_block(segment, rows, cols):
    width = rows + cols - 1
    turned = jnp.concatenate([segment[rows - 1:], segment[:rows - 1]])
    flat = jnp.broadcast_to(turned, (rows, width)).reshape(-1)[: rows * (width - 1)]
    return flat.reshape(rows, width - 1)[:, :cols]


def filter_series(signal, filters):
    taps = filters.shape[1]
    tout = signal.shape[0] - taps
    tblock = min(512, tout)
    kblock = min(512, taps)
    outputs = []
    for tpos in range(tout // tblock):
        pieces = []
        for kpos in range(taps // kblock):
            begin = tpos * tblock + taps - (kpos + 1) * kblock
            segment = signal[begin:begin + kblock + tblock - 1]
            pieces.append(toeplitz_block(segment, kblock, tblock))
        frame = jnp.concatenate(pieces, axis=0)
        outputs.append(jnp.dot(filters, frame, preferred_element_type=jnp.float32))
    return jnp.concatenate(outputs, axis=1)


def reference(strain, basis, recon):
    scale = 1.0 / (2.0 * NDET)

    def one_split(pair):
        filters, weights = pair
        series = jnp.stack([filter_series(strain[det], filters).astype(jnp.bfloat16) for det in range(NDET)])
        series_wide = series.astype(jnp.float32)
        mblock = min(512, TEMPLATES)
        blocks = []
        for mpos in range(TEMPLATES // mblock):
            part = weights[:, mpos * mblock:(mpos + 1) * mblock].astype(jnp.float32)
            total = jnp.zeros((mblock, TOUT), jnp.float32)
            for det in range(NDET):
                zvals = jnp.einsum("qml,lt->qmt", part, series_wide[det])
                total = total + jnp.sum(zvals * zvals, axis=0)
            blocks.append(total * scale)
        return jnp.concatenate(blocks, axis=0)

    snr2 = lax.map(one_split, (basis, recon))
    loudest = jnp.max(snr2, axis=(0, 1))
    return snr2, loudest
```

```python
import functools

import jax
import jax.numpy as jnp
from jax import lax
from jax.experimental import pallas as pl
from jax.experimental.pallas import tpu as pltpu
from jax.sharding import PartitionSpec as P

VMEM = pltpu.VMEM


def spread(block, axes, count):
    copies = jnp.broadcast_to(block[None], (count,) + block.shape)
    return lax.all_to_all(copies, axes, 0, 0, tiled=True)


def join_strain(parts_ref, det, piece):
    count = parts_ref.shape[0]
    part = parts_ref[:, det * piece : (det + 1) * piece].astype(jnp.float32)
    group = jnp.concatenate([part] * (128 // piece), axis=1)
    wide = jnp.concatenate([group] * (count * piece // 128), axis=1)
    owner = lax.broadcasted_iota(jnp.int32, wide.shape, 1) // piece
    mine = lax.broadcasted_iota(jnp.int32, wide.shape, 0)
    return jnp.sum(jnp.where(owner == mine, wide, 0.0), axis=0, keepdims=True)


def fill_slab(line, slab_ref, det):
    samples = line.shape[1]
    rows, cols = slab_ref.shape[1:]
    base = jnp.broadcast_to(line, (8, samples))
    first = pltpu.roll(base, samples - 7, 1, stride=1, stride_axis=0)
    turned = [first] + [pltpu.roll(first, samples - 8 * m, 1) for m in range(1, 16)]
    for m in range(1, 16, 2):
        pair = jnp.concatenate([turned[m], turned[m - 1]], axis=0).astype(jnp.bfloat16)
        for q in range(rows // 128):
            row = 16 * ((rows // 8 - 1 - 16 * q - m) // 2)
            slab_ref[det, row : row + 16, :] = pair[:, 128 * q : 128 * q + cols]


def bank_kernel(parts_ref, *refs, blocks, ndet, taps):
    block_refs = refs[:blocks]
    weights_ref, snr_ref, peak_ref, basis_ref, slab_ref, series_ref = refs[blocks:]
    step = pl.program_id(0)
    cols = slab_ref.shape[2]
    nbasis = basis_ref.shape[0]
    each = nbasis // blocks
    piece = parts_ref.shape[1] // ndet

    @pl.when(step == 0)
    def _():
        for det in range(ndet):
            fill_slab(join_strain(parts_ref, det, piece), slab_ref, det)
        for index in range(blocks):
            basis_ref[index * each : (index + 1) * each, :] = block_refs[index][...]
        series_ref[...] = jnp.zeros_like(series_ref)

    start = pl.multiple_of((pl.num_programs(0) - 1 - step) * cols, cols)
    templ = weights_ref.shape[0] // 2
    total = None
    for det in range(ndet):
        frame = slab_ref[det, pl.ds(start, taps), :]
        series = jnp.dot(basis_ref[...], frame, preferred_element_type=jnp.float32)
        series_ref[det, :nbasis, :] = series.astype(jnp.bfloat16)
        zvals = jnp.dot(weights_ref[...], series_ref[det], preferred_element_type=jnp.float32)
        power = zvals * zvals
        both = power[:templ] + power[templ:]
        total = both if total is None else total + both
    snr = total * (1.0 / (2.0 * ndet))
    snr_ref[...] = snr
    peak_ref[...] = jnp.max(snr, axis=0, keepdims=True)


def bank(parts, blocks, weights, ndet, cols):
    samples = parts.shape[0] * parts.shape[1] // ndet
    taps = blocks[0].shape[1]
    tout = samples - taps
    nbasis = sum(block.shape[0] for block in blocks)
    templ, depth = weights.shape[0] // 2, weights.shape[1]
    body = functools.partial(bank_kernel, blocks=len(blocks), ndet=ndet, taps=taps)
    flops = 2 * ndet * tout * (nbasis * taps + 2 * templ * nbasis)
    return pl.pallas_call(
        body,
        grid=(tout // cols,),
        in_specs=[pl.BlockSpec(memory_space=VMEM)] * (len(blocks) + 2),
        out_specs=[
            pl.BlockSpec((templ, cols), lambda i: (0, i)),
            pl.BlockSpec((1, cols), lambda i: (0, i)),
        ],
        out_shape=[
            jax.ShapeDtypeStruct((templ, tout), jnp.float32),
            jax.ShapeDtypeStruct((1, tout), jnp.float32),
        ],
        scratch_shapes=[
            VMEM((nbasis, taps), jnp.bfloat16),
            VMEM((ndet, samples - cols, cols), jnp.bfloat16),
            VMEM((ndet, depth, cols), jnp.bfloat16),
        ],
        compiler_params=pltpu.CompilerParams(vmem_limit_bytes=32 << 20),
        cost_estimate=pl.CostEstimate(
            flops=flops, bytes_accessed=4 * templ * tout + 2 * nbasis * taps, transcendentals=0
        ),
    )(parts, *blocks, weights)


def per_device(strain, basis, recon, nsplit, nshard):
    own = basis[0]
    ndet = strain.shape[0]
    each = own.shape[0]
    me = lax.axis_index("shard")

    blocks = [own]
    for away in range(1, nshard):
        pairs = [(i, i ^ away) for i in range(nshard)]
        blocks.append(lax.ppermute(own, "shard", pairs))
    parts = spread(strain.reshape(-1), ("split", "shard"), nsplit * nshard)

    nbasis = each * nshard
    depth = -(-nbasis // 256) * 256
    col = lax.broadcasted_iota(jnp.int32, (nbasis, depth), 1)
    source = ((col // each) ^ me) * each + col % each
    row = lax.broadcasted_iota(jnp.int32, (nbasis, depth), 0)
    order = ((row == source) & (col < nbasis)).astype(jnp.bfloat16)
    weights = jnp.einsum("qml,lp->qmp", recon[0], order, preferred_element_type=jnp.float32)
    weights = weights.astype(jnp.bfloat16).reshape(-1, depth)

    snr, peak = bank(parts, blocks, weights, ndet, 512)

    peak = peak.reshape(-1)
    peak = jnp.max(spread(peak, "shard", nshard), axis=0)
    loudest = jnp.max(spread(peak, "split", nsplit), axis=0)
    return (snr[None], loudest)


def solution(mesh):
    body = functools.partial(
        per_device, nsplit=mesh.shape["split"], nshard=mesh.shape["shard"]
    )
    return jax.shard_map(
        body,
        mesh=mesh,
        in_specs=(
            P(None, ("split", "shard")),
            P("split", "shard", None),
            P("split", None, "shard", None),
        ),
        out_specs=(P("split", "shard", None), P()),
        check_vma=False,
    )
```

```python
import functools

import jax
import jax.numpy as jnp
from jax import lax
from jax.experimental import pallas as pl
from jax.experimental.pallas import tpu as pltpu
from jax.sharding import PartitionSpec as P

VMEM = pltpu.VMEM
LIMIT = 30 << 20
COLS = 512
EARLY = 4


def spread(block, axes, count):
    copies = jnp.broadcast_to(block[None], (count,) + block.shape)
    return lax.all_to_all(copies, axes, 0, 0, tiled=True)


def join_strain(parts_ref, lines_ref, turned_ref):
    ndet = lines_ref.shape[0]
    count, piece = parts_ref.shape[0], parts_ref.shape[1] // ndet
    side = 128 // piece
    rows = count // side
    for det in range(ndet):
        cut = slice(det * piece, (det + 1) * piece)
        quarters = [parts_ref[pl.ds(j, rows, stride=side), :][:, cut] for j in range(side)]
        turned_ref[...] = jnp.concatenate(quarters, axis=1)
        for row in range(rows):
            lines_ref[det : det + 1, 128 * row : 128 * row + 128] = turned_ref[row : row + 1, :]


def fill_slab(line, slab_ref, det):
    samples = line.shape[1]
    rows, cols = slab_ref.shape[1:]
    base = jnp.broadcast_to(line, (8, samples))
    first = pltpu.roll(base, samples - 7, 1, stride=1, stride_axis=0)
    turned = [first] + [pltpu.roll(first, samples - 8 * m, 1) for m in range(1, 16)]
    for m in range(1, 16, 2):
        pair = jnp.concatenate([turned[m], turned[m - 1]], axis=0).astype(jnp.bfloat16)
        for q in range(rows // 128):
            row = 16 * ((rows // 8 - 1 - 16 * q - m) // 2)
            slab_ref[det, row : row + 16, :] = pair[:, 128 * q : 128 * q + cols]


def prepare(lines_ref, block_refs, slab_ref, basis_ref):
    for det in range(slab_ref.shape[0]):
        fill_slab(lines_ref[det : det + 1, :], slab_ref, det)
    row = 0
    for block_ref in block_refs:
        each = block_ref.shape[0]
        basis_ref[row : row + each, :] = block_ref[...]
        row += each


def filtered(basis_ref, slab_ref, det, step, steps):
    taps, cols = basis_ref.shape[1], slab_ref.shape[2]
    start = pl.multiple_of((steps - 1 - step) * cols, cols)
    frame = slab_ref[det, pl.ds(start, taps), :]
    return jnp.dot(basis_ref[...], frame, preferred_element_type=jnp.float32).astype(jnp.bfloat16)


def early_kernel(parts_ref, *refs, blocks):
    block_refs = refs[:blocks]
    out_ref, lines_ref, basis_ref, slab_ref, turned_ref = refs[blocks:]
    step = pl.program_id(0)

    @pl.when(step == 0)
    def _():
        join_strain(parts_ref, lines_ref, turned_ref)
        prepare(lines_ref, block_refs, slab_ref, basis_ref)

    for det in range(out_ref.shape[0]):
        out_ref[det] = filtered(basis_ref, slab_ref, det, step, pl.num_programs(0))


def late_kernel(lines_ref, early_ref, weights_ref, *refs, blocks):
    block_refs = refs[:blocks]
    snr_ref, peak_ref, basis_ref, slab_ref, series_ref = refs[blocks:]
    step, steps = pl.program_id(0), pl.num_programs(0)
    ndet, nearly = early_ref.shape[:2]
    nlate = basis_ref.shape[0]

    @pl.when(step == 0)
    def _():
        prepare(lines_ref, block_refs, slab_ref, basis_ref)
        series_ref[...] = jnp.zeros_like(series_ref)

    templ = weights_ref.shape[0] // 2

    def fill(det):
        series_ref[det, :nearly, :] = early_ref[det]
        late = filtered(basis_ref, slab_ref, det, step, steps)
        series_ref[det, nearly : nearly + nlate, :] = late

    total = None
    fill(0)
    for det in range(ndet):
        if det + 1 < ndet:
            fill(det + 1)
        zvals = jnp.dot(weights_ref[...], series_ref[det], preferred_element_type=jnp.float32)
        power = zvals * zvals
        both = power[:templ] + power[templ:]
        total = both if total is None else total + both
    snr = total * (1.0 / (2.0 * ndet))
    snr_ref[...] = snr
    peak_ref[...] = jnp.max(snr, axis=0, keepdims=True)


def early_series(parts, blocks, ndet):
    samples = parts.size // ndet
    taps = blocks[0].shape[1]
    tout = samples - taps
    nearly = sum(block.shape[0] for block in blocks)
    return pl.pallas_call(
        functools.partial(early_kernel, blocks=len(blocks)),
        grid=(tout // COLS,),
        in_specs=[pl.BlockSpec(memory_space=VMEM)] * (len(blocks) + 1),
        out_specs=[
            pl.BlockSpec((ndet, nearly, COLS), lambda i: (0, 0, i)),
            pl.BlockSpec((ndet, samples), lambda i: (0, 0)),
        ],
        out_shape=[
            jax.ShapeDtypeStruct((ndet, nearly, tout), jnp.bfloat16),
            jax.ShapeDtypeStruct((ndet, samples), jnp.float32),
        ],
        scratch_shapes=[
            VMEM((nearly, taps), jnp.bfloat16),
            VMEM((ndet, samples - COLS, COLS), jnp.bfloat16),
            VMEM((samples // 128, 128), jnp.float32),
        ],
        compiler_params=pltpu.CompilerParams(vmem_limit_bytes=LIMIT),
    )(parts, *blocks)


def bank(lines, early, blocks, weights):
    ndet, nearly, tout = early.shape
    taps = blocks[0].shape[1]
    samples = tout + taps
    nlate = sum(block.shape[0] for block in blocks)
    templ, depth = weights.shape[0] // 2, weights.shape[1]
    steps = tout // COLS
    whole = pl.BlockSpec(memory_space=VMEM)
    return pl.pallas_call(
        functools.partial(late_kernel, blocks=len(blocks)),
        grid=(steps,),
        in_specs=[whole, pl.BlockSpec((ndet, nearly, COLS), lambda i: (0, 0, i)), whole]
        + [whole] * len(blocks),
        out_specs=[
            pl.BlockSpec((templ, COLS), lambda i: (0, i)),
            pl.BlockSpec((1, COLS), lambda i: (0, i)),
        ],
        out_shape=[
            jax.ShapeDtypeStruct((templ, tout), jnp.float32),
            jax.ShapeDtypeStruct((1, tout), jnp.float32),
        ],
        scratch_shapes=[
            VMEM((nlate, taps), jnp.bfloat16),
            VMEM((ndet, samples - COLS, COLS), jnp.bfloat16),
            VMEM((ndet, depth, COLS), jnp.bfloat16),
        ],
        compiler_params=pltpu.CompilerParams(vmem_limit_bytes=LIMIT),
    )(lines, early, weights, *blocks)


def per_device(strain, basis, recon, nsplit, nshard):
    own = basis[0]
    each = own.shape[0]
    count = nsplit * nshard
    me = lax.axis_index("shard")

    parts = spread(strain.astype(jnp.float32).reshape(-1), ("split", "shard"), count)

    def swap(block, away):
        pairs = [(i, i ^ away) for i in range(nshard)]
        return lax.ppermute(block, "shard", pairs)

    got = {0: own}
    for away in (4, 1, 3, 2):
        got[away] = swap(own, away)
    got[5] = swap(got[4], 1)
    got[7] = swap(got[4], 3)
    got[6] = swap(got[2], 4)
    far = [0, 4, 1, 3, 2, 5, 7, 6]
    blocks = [got[away] for away in far]

    nbasis = each * nshard
    depth = -(-nbasis // 256) * 256
    col = lax.broadcasted_iota(jnp.int32, (nbasis, depth), 1)
    row = lax.broadcasted_iota(jnp.int32, (nbasis, depth), 0)
    away = jnp.zeros((nbasis, depth), jnp.int32)
    for place, distance in enumerate(far):
        away = jnp.where(col // each == place, distance, away)
    source = (away ^ me) * each + col % each
    order = ((row == source) & (col < nbasis)).astype(jnp.bfloat16)
    weights = jnp.einsum("qml,lp->qmp", recon[0], order, preferred_element_type=jnp.float32)
    weights = weights.astype(jnp.bfloat16).reshape(-1, depth)

    early, lines = early_series(parts, blocks[:EARLY], strain.shape[0])
    snr, peak = bank(lines, early, blocks[EARLY:], weights)

    peak = jnp.max(spread(peak.reshape(-1), "shard", nshard), axis=0)
    loudest = jnp.max(spread(peak, "split", nsplit), axis=0)
    return (snr[None], loudest)


def solution(mesh):
    body = functools.partial(
        per_device, nsplit=mesh.shape["split"], nshard=mesh.shape["shard"]
    )
    return jax.shard_map(
        body,
        mesh=mesh,
        in_specs=(
            P(None, ("split", "shard")),
            P("split", "shard", None),
            P("split", None, "shard", None),
        ),
        out_specs=(P("split", "shard", None), P()),
        check_vma=False,
    )
```

```python
import functools

import jax
import jax.numpy as jnp
from jax import lax
from jax.experimental import pallas as pl
from jax.experimental.pallas import tpu as pltpu
from jax.sharding import PartitionSpec as P

VMEM = pltpu.VMEM
LIMIT = 30 << 20
COLS = 512
EARLY = 3


def spread(block, axes, count):
    copies = jnp.broadcast_to(block[None], (count,) + block.shape)
    return lax.all_to_all(copies, axes, 0, 0, tiled=True)


def join_strain(parts_ref, lines_ref, turned_ref):
    ndet = lines_ref.shape[0]
    count, piece = parts_ref.shape[0], parts_ref.shape[1] // ndet
    side = 128 // piece
    rows = count // side
    for det in range(ndet):
        cut = slice(det * piece, (det + 1) * piece)
        quarters = [parts_ref[pl.ds(j, rows, stride=side), :][:, cut] for j in range(side)]
        turned_ref[...] = jnp.concatenate(quarters, axis=1)
        for row in range(rows):
            lines_ref[det : det + 1, 128 * row : 128 * row + 128] = turned_ref[row : row + 1, :]


def fill_slab(line, slab_ref, det):
    samples = line.shape[1]
    rows, cols = slab_ref.shape[1:]
    base = jnp.broadcast_to(line, (8, samples))
    first = pltpu.roll(base, samples - 7, 1, stride=1, stride_axis=0)
    turned = [first] + [pltpu.roll(first, samples - 8 * m, 1) for m in range(1, 16)]
    for m in range(1, 16, 2):
        pair = jnp.concatenate([turned[m], turned[m - 1]], axis=0).astype(jnp.bfloat16)
        for q in range(rows // 128):
            row = 16 * ((rows // 8 - 1 - 16 * q - m) // 2)
            slab_ref[det, row : row + 16, :] = pair[:, 128 * q : 128 * q + cols]


def stack_blocks(block_refs, basis_ref):
    row = 0
    for block_ref in block_refs:
        each = block_ref.shape[0]
        basis_ref[row : row + each, :] = block_ref[...]
        row += each


def filtered(basis_ref, slab_ref, det, step, steps):
    taps, cols = basis_ref.shape[1], slab_ref.shape[2]
    start = pl.multiple_of((steps - 1 - step) * cols, cols)
    frame = slab_ref[det, pl.ds(start, taps), :]
    return jnp.dot(basis_ref[...], frame, preferred_element_type=jnp.float32).astype(jnp.bfloat16)


def early_kernel(parts_ref, *refs, blocks):
    block_refs = refs[:blocks]
    out_ref, slab_ref, lines_ref, basis_ref, turned_ref = refs[blocks:]
    step = pl.program_id(0)

    @pl.when(step == 0)
    def _():
        join_strain(parts_ref, lines_ref, turned_ref)
        for det in range(slab_ref.shape[0]):
            fill_slab(lines_ref[det : det + 1, :], slab_ref, det)
        stack_blocks(block_refs, basis_ref)

    for det in range(out_ref.shape[0]):
        out_ref[det] = filtered(basis_ref, slab_ref, det, step, pl.num_programs(0))


def late_kernel(slab_ref, early_ref, weights_ref, *refs, blocks):
    block_refs = refs[:blocks]
    snr_ref, peak_ref, basis_ref, series_ref = refs[blocks:]
    step, steps = pl.program_id(0), pl.num_programs(0)
    ndet, nearly = early_ref.shape[:2]
    nlate = basis_ref.shape[0]

    @pl.when(step == 0)
    def _():
        stack_blocks(block_refs, basis_ref)
        series_ref[...] = jnp.zeros_like(series_ref)

    templ = weights_ref.shape[0] // 2

    def fill(det):
        series_ref[det, :nearly, :] = early_ref[det]
        late = filtered(basis_ref, slab_ref, det, step, steps)
        series_ref[det, nearly : nearly + nlate, :] = late

    total = None
    fill(0)
    for det in range(ndet):
        if det + 1 < ndet:
            fill(det + 1)
        zvals = jnp.dot(weights_ref[...], series_ref[det], preferred_element_type=jnp.float32)
        power = zvals * zvals
        both = power[:templ] + power[templ:]
        total = both if total is None else total + both
    snr = total * (1.0 / (2.0 * ndet))
    snr_ref[...] = snr
    peak_ref[...] = jnp.max(snr, axis=0, keepdims=True)


def early_series(parts, blocks, ndet):
    samples = parts.size // ndet
    taps = blocks[0].shape[1]
    tout = samples - taps
    nearly = sum(block.shape[0] for block in blocks)
    return pl.pallas_call(
        functools.partial(early_kernel, blocks=len(blocks)),
        grid=(tout // COLS,),
        in_specs=[pl.BlockSpec(memory_space=VMEM)] * (len(blocks) + 1),
        out_specs=[
            pl.BlockSpec((ndet, nearly, COLS), lambda i: (0, 0, i)),
            pl.BlockSpec(memory_space=VMEM),
        ],
        out_shape=[
            jax.ShapeDtypeStruct((ndet, nearly, tout), jnp.bfloat16),
            jax.ShapeDtypeStruct((ndet, samples - COLS, COLS), jnp.bfloat16),
        ],
        scratch_shapes=[
            VMEM((ndet, samples), jnp.float32),
            VMEM((nearly, taps), jnp.bfloat16),
            VMEM((samples // 128, 128), jnp.float32),
        ],
        compiler_params=pltpu.CompilerParams(vmem_limit_bytes=LIMIT),
    )(parts, *blocks)


def bank(slab, early, blocks, weights):
    ndet, nearly, tout = early.shape
    taps = blocks[0].shape[1]
    nlate = sum(block.shape[0] for block in blocks)
    templ, depth = weights.shape[0] // 2, weights.shape[1]
    steps = tout // COLS
    whole = pl.BlockSpec(memory_space=VMEM)
    return pl.pallas_call(
        functools.partial(late_kernel, blocks=len(blocks)),
        grid=(steps,),
        in_specs=[whole, pl.BlockSpec((ndet, nearly, COLS), lambda i: (0, 0, i)), whole]
        + [whole] * len(blocks),
        out_specs=[
            pl.BlockSpec((templ, COLS), lambda i: (0, i)),
            pl.BlockSpec((1, COLS), lambda i: (0, i)),
        ],
        out_shape=[
            jax.ShapeDtypeStruct((templ, tout), jnp.float32),
            jax.ShapeDtypeStruct((1, tout), jnp.float32),
        ],
        scratch_shapes=[
            VMEM((nlate, taps), jnp.bfloat16),
            VMEM((ndet, depth, COLS), jnp.bfloat16),
        ],
        compiler_params=pltpu.CompilerParams(vmem_limit_bytes=LIMIT),
    )(slab, early, weights, *blocks)


def per_device(strain, basis, recon, nsplit, nshard):
    own = basis[0]
    each = own.shape[0]
    count = nsplit * nshard
    me = lax.axis_index("shard")

    parts = spread(strain.astype(jnp.float32).reshape(-1), ("split", "shard"), count)

    def swap(block, away):
        pairs = [(i, i ^ away) for i in range(nshard)]
        return lax.ppermute(block, "shard", pairs)

    got = {0: own, 4: swap(own, 4), 2: swap(own, 2)}
    got[6] = swap(got[2], 4)
    later, _ = lax.optimization_barrier((own, got[4]))
    got[1], got[3] = swap(later, 1), swap(later, 3)
    got[5], got[7] = swap(got[4], 1), swap(got[4], 3)
    far = [0, 4, 2, 6, 1, 3, 5, 7]
    blocks = [got[away] for away in far]

    nbasis = each * nshard
    depth = -(-nbasis // 256) * 256
    col = lax.broadcasted_iota(jnp.int32, (nbasis, depth), 1)
    row = lax.broadcasted_iota(jnp.int32, (nbasis, depth), 0)
    away = jnp.zeros((nbasis, depth), jnp.int32)
    for place, distance in enumerate(far):
        away = jnp.where(col // each == place, distance, away)
    source = (away ^ me) * each + col % each
    order = ((row == source) & (col < nbasis)).astype(jnp.bfloat16)
    weights = jnp.einsum("qml,lp->qmp", recon[0], order, preferred_element_type=jnp.float32)
    weights = weights.astype(jnp.bfloat16).reshape(-1, depth)

    early, slab = early_series(parts, blocks[:EARLY], strain.shape[0])
    snr, peak = bank(slab, early, blocks[EARLY:], weights)

    peak = jnp.max(spread(peak.reshape(-1), "shard", nshard), axis=0)
    loudest = jnp.max(spread(peak, "split", nsplit), axis=0)
    return (snr[None], loudest)


def solution(mesh):
    body = functools.partial(
        per_device, nsplit=mesh.shape["split"], nshard=mesh.shape["shard"]
    )
    return jax.shard_map(
        body,
        mesh=mesh,
        in_specs=(
            P(None, ("split", "shard")),
            P("split", "shard", None),
            P("split", None, "shard", None),
        ),
        out_specs=(P("split", "shard", None), P()),
        check_vma=False,
    )
```

```python
import functools

import jax
import jax.numpy as jnp
from jax import lax
from jax.experimental import pallas as pl
from jax.experimental.pallas import tpu as pltpu
from jax.sharding import PartitionSpec as P

VMEM = pltpu.VMEM
LIMIT = 30 << 20
COLS = 512
EARLY = 3


def spread(block, axes, count):
    copies = jnp.broadcast_to(block[None], (count,) + block.shape)
    return lax.all_to_all(copies, axes, 0, 0, tiled=True)


def join_strain(parts_ref, lines_ref, turned_ref):
    ndet = lines_ref.shape[0]
    count, piece = parts_ref.shape[0], parts_ref.shape[1] // ndet
    side = 128 // piece
    rows = count // side
    for det in range(ndet):
        cut = slice(det * piece, (det + 1) * piece)
        quarters = [parts_ref[pl.ds(j, rows, stride=side), :][:, cut] for j in range(side)]
        turned_ref[...] = jnp.concatenate(quarters, axis=1)
        for row in range(rows):
            lines_ref[det : det + 1, 128 * row : 128 * row + 128] = turned_ref[row : row + 1, :]


def fill_slab(line, slab_ref, det):
    samples = line.shape[1]
    rows, cols = slab_ref.shape[1:]
    base = jnp.broadcast_to(line, (8, samples))
    first = pltpu.roll(base, samples - 7, 1, stride=1, stride_axis=0)
    turned = [first] + [pltpu.roll(first, samples - 8 * m, 1) for m in range(1, 16)]
    for m in range(1, 16, 2):
        pair = jnp.concatenate([turned[m], turned[m - 1]], axis=0).astype(jnp.bfloat16)
        for q in range(rows // 128):
            row = 16 * ((rows // 8 - 1 - 16 * q - m) // 2)
            slab_ref[det, row : row + 16, :] = pair[:, 128 * q : 128 * q + cols]


def stack_blocks(block_refs, basis_ref):
    row = 0
    for block_ref in block_refs:
        each = block_ref.shape[0]
        basis_ref[row : row + each, :] = block_ref[...]
        row += each


def filtered(basis_ref, slab_ref, det, step, steps):
    taps, cols = basis_ref.shape[1], slab_ref.shape[2]
    start = pl.multiple_of((steps - 1 - step) * cols, cols)
    frame = slab_ref[det, pl.ds(start, taps), :]
    return jnp.dot(basis_ref[...], frame, preferred_element_type=jnp.float32).astype(jnp.bfloat16)


def early_kernel(parts_ref, *refs, blocks):
    block_refs = refs[:blocks]
    out_ref, slab_ref, lines_ref, basis_ref, turned_ref = refs[blocks:]
    step = pl.program_id(0)

    @pl.when(step == 0)
    def _():
        join_strain(parts_ref, lines_ref, turned_ref)
        for det in range(slab_ref.shape[0]):
            fill_slab(lines_ref[det : det + 1, :], slab_ref, det)
        stack_blocks(block_refs, basis_ref)

    for det in range(out_ref.shape[0]):
        out_ref[det] = filtered(basis_ref, slab_ref, det, step, pl.num_programs(0))


def late_kernel(slab_ref, early_ref, weights_ref, *refs, blocks):
    block_refs = refs[:blocks]
    snr_ref, peak_ref, basis_ref, series_ref = refs[blocks:]
    step, steps = pl.program_id(0), pl.num_programs(0)
    ndet, nearly = early_ref.shape[:2]
    nlate = basis_ref.shape[0]

    @pl.when(step == 0)
    def _():
        stack_blocks(block_refs, basis_ref)

    templ = weights_ref.shape[0] // 2

    def fill(det):
        series_ref[det, :nearly, :] = early_ref[det]
        late = filtered(basis_ref, slab_ref, det, step, steps)
        series_ref[det, nearly : nearly + nlate, :] = late

    nbasis = nearly + nlate
    total = None
    fill(0)
    for det in range(ndet):
        if det + 1 < ndet:
            fill(det + 1)
        for quad in range(2):
            rows = weights_ref[quad * templ : (quad + 1) * templ, :nbasis]
            zvals = jnp.dot(rows, series_ref[det], preferred_element_type=jnp.float32)
            total = zvals * zvals if total is None else total + zvals * zvals
    snr = total * (1.0 / (2.0 * ndet))
    snr_ref[...] = snr
    peak_ref[...] = jnp.max(snr, axis=0, keepdims=True)


def early_series(parts, blocks, ndet):
    samples = parts.size // ndet
    taps = blocks[0].shape[1]
    tout = samples - taps
    nearly = sum(block.shape[0] for block in blocks)
    return pl.pallas_call(
        functools.partial(early_kernel, blocks=len(blocks)),
        grid=(tout // COLS,),
        in_specs=[pl.BlockSpec(memory_space=VMEM)] * (len(blocks) + 1),
        out_specs=[
            pl.BlockSpec((ndet, nearly, COLS), lambda i: (0, 0, i)),
            pl.BlockSpec(memory_space=VMEM),
        ],
        out_shape=[
            jax.ShapeDtypeStruct((ndet, nearly, tout), jnp.bfloat16),
            jax.ShapeDtypeStruct((ndet, samples - COLS, COLS), jnp.bfloat16),
        ],
        scratch_shapes=[
            VMEM((ndet, samples), jnp.float32),
            VMEM((nearly, taps), jnp.bfloat16),
            VMEM((samples // 128, 128), jnp.float32),
        ],
        compiler_params=pltpu.CompilerParams(vmem_limit_bytes=LIMIT),
    )(parts, *blocks)


def bank(slab, early, blocks, weights):
    ndet, nearly, tout = early.shape
    taps = blocks[0].shape[1]
    nlate = sum(block.shape[0] for block in blocks)
    templ = weights.shape[0] // 2
    steps = tout // COLS
    whole = pl.BlockSpec(memory_space=VMEM)
    return pl.pallas_call(
        functools.partial(late_kernel, blocks=len(blocks)),
        grid=(steps,),
        in_specs=[whole, pl.BlockSpec((ndet, nearly, COLS), lambda i: (0, 0, i)), whole]
        + [whole] * len(blocks),
        out_specs=[
            pl.BlockSpec((templ, COLS), lambda i: (0, i)),
            pl.BlockSpec((1, COLS), lambda i: (0, i)),
        ],
        out_shape=[
            jax.ShapeDtypeStruct((templ, tout), jnp.float32),
            jax.ShapeDtypeStruct((1, tout), jnp.float32),
        ],
        scratch_shapes=[
            VMEM((nlate, taps), jnp.bfloat16),
            VMEM((ndet, nearly + nlate, COLS), jnp.bfloat16),
        ],
        compiler_params=pltpu.CompilerParams(vmem_limit_bytes=LIMIT),
    )(slab, early, weights, *blocks)


def copy_kernel(strain_ref, copies_ref):
    ndet, piece = strain_ref.shape
    for det in range(ndet):
        row = strain_ref[det : det + 1, :].astype(jnp.float32)
        copies_ref[:, det * piece : (det + 1) * piece] = jnp.broadcast_to(
            row, (copies_ref.shape[0], piece)
        )


def strain_copies(strain, count):
    return pl.pallas_call(
        copy_kernel,
        in_specs=[pl.BlockSpec(memory_space=VMEM)],
        out_specs=pl.BlockSpec(memory_space=VMEM),
        out_shape=jax.ShapeDtypeStruct((count, strain.size), jnp.float32),
        compiler_params=pltpu.CompilerParams(vmem_limit_bytes=LIMIT),
    )(strain)


def per_device(strain, basis, recon, nsplit, nshard):
    own = basis[0]
    each = own.shape[0]
    count = nsplit * nshard
    me = lax.axis_index("shard")

    copies = strain_copies(strain, count)
    parts = lax.all_to_all(copies, ("split", "shard"), 0, 0, tiled=True)

    def swap(block, away):
        pairs = [(i, i ^ away) for i in range(nshard)]
        return lax.ppermute(block, "shard", pairs)

    got = {0: own, 4: swap(own, 4), 2: swap(own, 2)}
    got[6] = swap(got[2], 4)
    later, _ = lax.optimization_barrier((own, got[4]))
    got[1], got[3] = swap(later, 1), swap(later, 3)
    got[5], got[7] = swap(got[4], 1), swap(got[4], 3)
    far = [0, 4, 2, 6, 1, 3, 5, 7]
    blocks = [got[away] for away in far]

    nbasis = each * nshard
    depth = -(-nbasis // 256) * 256
    col = lax.broadcasted_iota(jnp.int32, (nbasis, depth), 1)
    row = lax.broadcasted_iota(jnp.int32, (nbasis, depth), 0)
    away = jnp.zeros((nbasis, depth), jnp.int32)
    for place, distance in enumerate(far):
        away = jnp.where(col // each == place, distance, away)
    source = (away ^ me) * each + col % each
    order = ((row == source) & (col < nbasis)).astype(jnp.bfloat16)
    weights = jnp.einsum("qml,lp->qmp", recon[0], order, preferred_element_type=jnp.float32)
    weights = weights.astype(jnp.bfloat16).reshape(-1, depth)

    early, slab = early_series(parts, blocks[:EARLY], strain.shape[0])
    snr, peak = bank(slab, early, blocks[EARLY:], weights)

    peak = jnp.max(spread(peak.reshape(-1), "shard", nshard), axis=0)
    loudest = jnp.max(spread(peak, "split", nsplit), axis=0)
    return (snr[None], loudest)


def solution(mesh):
    body = functools.partial(
        per_device, nsplit=mesh.shape["split"], nshard=mesh.shape["shard"]
    )
    return jax.shard_map(
        body,
        mesh=mesh,
        in_specs=(
            P(None, ("split", "shard")),
            P("split", "shard", None),
            P("split", None, "shard", None),
        ),
        out_specs=(P("split", "shard", None), P()),
        check_vma=False,
    )
```

```python
import functools

import jax
import jax.numpy as jnp
from jax import lax
from jax.experimental import pallas as pl
from jax.experimental.pallas import tpu as pltpu
from jax.sharding import PartitionSpec as P

VMEM = pltpu.VMEM
LIMIT = 30 << 20
COLS = 512
EARLY = 3


def spread(block, axes, count):
    copies = jnp.broadcast_to(block[None], (count,) + block.shape)
    return lax.all_to_all(copies, axes, 0, 0, tiled=True)


def join_strain(parts_ref, lines_ref, turned_ref):
    ndet = lines_ref.shape[0]
    count, piece = parts_ref.shape[0], parts_ref.shape[1] // ndet
    side = 128 // piece
    rows = count // side
    for det in range(ndet):
        cut = slice(det * piece, (det + 1) * piece)
        quarters = [parts_ref[pl.ds(j, rows, stride=side), :][:, cut] for j in range(side)]
        turned_ref[...] = jnp.concatenate(quarters, axis=1)
        for row in range(rows):
            lines_ref[det : det + 1, 128 * row : 128 * row + 128] = turned_ref[row : row + 1, :]


def fill_slab(line, slab_ref, det):
    samples = line.shape[1]
    rows, cols = slab_ref.shape[1:]
    base = jnp.broadcast_to(line, (8, samples))
    first = pltpu.roll(base, samples - 7, 1, stride=1, stride_axis=0)
    turned = [first] + [pltpu.roll(first, samples - 8 * m, 1) for m in range(1, 16)]
    for m in range(1, 16, 2):
        pair = jnp.concatenate([turned[m], turned[m - 1]], axis=0).astype(jnp.bfloat16)
        for q in range(rows // 128):
            row = 16 * ((rows // 8 - 1 - 16 * q - m) // 2)
            slab_ref[det, row : row + 16, :] = pair[:, 128 * q : 128 * q + cols]


def stack_blocks(block_refs, basis_ref):
    row = 0
    for block_ref in block_refs:
        each = block_ref.shape[0]
        basis_ref[row : row + each, :] = block_ref[...]
        row += each


def filtered(basis_ref, slab_ref, det, step, steps):
    taps, cols = basis_ref.shape[1], slab_ref.shape[2]
    start = pl.multiple_of((steps - 1 - step) * cols, cols)
    frame = slab_ref[det, pl.ds(start, taps), :]
    return jnp.dot(basis_ref[...], frame, preferred_element_type=jnp.float32).astype(jnp.bfloat16)


def early_kernel(parts_ref, *refs, blocks):
    block_refs = refs[:blocks]
    out_ref, slab_ref, lines_ref, basis_ref, turned_ref = refs[blocks:]
    step = pl.program_id(0)

    @pl.when(step == 0)
    def _():
        join_strain(parts_ref, lines_ref, turned_ref)
        for det in range(slab_ref.shape[0]):
            fill_slab(lines_ref[det : det + 1, :], slab_ref, det)
        stack_blocks(block_refs, basis_ref)

    for det in range(out_ref.shape[0]):
        out_ref[det] = filtered(basis_ref, slab_ref, det, step, pl.num_programs(0))


def late_kernel(slab_ref, early_ref, weights_ref, *refs, blocks):
    block_refs = refs[:blocks]
    snr_ref, peak_ref, basis_ref, series_ref = refs[blocks:]
    step, steps = pl.program_id(0), pl.num_programs(0)
    ndet, nearly = early_ref.shape[:2]
    nlate = basis_ref.shape[0]

    @pl.when(step == 0)
    def _():
        stack_blocks(block_refs, basis_ref)

    templ = weights_ref.shape[0] // 2

    def fill(det):
        series_ref[det, :nearly, :] = early_ref[det]
        late = filtered(basis_ref, slab_ref, det, step, steps)
        series_ref[det, nearly : nearly + nlate, :] = late

    nbasis = nearly + nlate
    total = None
    fill(0)
    for det in range(ndet):
        if det + 1 < ndet:
            fill(det + 1)
        for quad in range(2):
            rows = weights_ref[quad * templ : (quad + 1) * templ, :nbasis]
            zvals = jnp.dot(rows, series_ref[det], preferred_element_type=jnp.float32)
            total = zvals * zvals if total is None else total + zvals * zvals
    snr = total * (1.0 / (2.0 * ndet))
    snr_ref[...] = snr
    peak_ref[...] = jnp.max(snr, axis=0, keepdims=True)


def early_series(parts, blocks, ndet):
    samples = parts.size // ndet
    taps = blocks[0].shape[1]
    tout = samples - taps
    nearly = sum(block.shape[0] for block in blocks)
    return pl.pallas_call(
        functools.partial(early_kernel, blocks=len(blocks)),
        grid=(tout // COLS,),
        in_specs=[pl.BlockSpec(memory_space=VMEM)] * (len(blocks) + 1),
        out_specs=[
            pl.BlockSpec((ndet, nearly, COLS), lambda i: (0, 0, i)),
            pl.BlockSpec(memory_space=VMEM),
        ],
        out_shape=[
            jax.ShapeDtypeStruct((ndet, nearly, tout), jnp.bfloat16),
            jax.ShapeDtypeStruct((ndet, samples - COLS, COLS), jnp.bfloat16),
        ],
        scratch_shapes=[
            VMEM((ndet, samples), jnp.float32),
            VMEM((nearly, taps), jnp.bfloat16),
            VMEM((samples // 128, 128), jnp.float32),
        ],
        compiler_params=pltpu.CompilerParams(vmem_limit_bytes=LIMIT),
    )(parts, *blocks)


def bank(slab, early, blocks, weights):
    ndet, nearly, tout = early.shape
    taps = blocks[0].shape[1]
    nlate = sum(block.shape[0] for block in blocks)
    templ = weights.shape[0] // 2
    steps = tout // COLS
    whole = pl.BlockSpec(memory_space=VMEM)
    return pl.pallas_call(
        functools.partial(late_kernel, blocks=len(blocks)),
        grid=(steps,),
        in_specs=[whole, pl.BlockSpec((ndet, nearly, COLS), lambda i: (0, 0, i)), whole]
        + [whole] * len(blocks),
        out_specs=[
            pl.BlockSpec((templ, COLS), lambda i: (0, i)),
            pl.BlockSpec((1, COLS), lambda i: (0, i)),
        ],
        out_shape=[
            jax.ShapeDtypeStruct((templ, tout), jnp.float32),
            jax.ShapeDtypeStruct((1, tout), jnp.float32),
        ],
        scratch_shapes=[
            VMEM((nlate, taps), jnp.bfloat16),
            VMEM((ndet, nearly + nlate, COLS), jnp.bfloat16),
        ],
        compiler_params=pltpu.CompilerParams(vmem_limit_bytes=LIMIT),
    )(slab, early, weights, *blocks)


def copy_kernel(strain_ref, copies_ref):
    ndet, piece = strain_ref.shape
    for det in range(ndet):
        row = strain_ref[det : det + 1, :].astype(jnp.float32)
        copies_ref[:, det * piece : (det + 1) * piece] = jnp.broadcast_to(
            row, (copies_ref.shape[0], piece)
        )


def strain_copies(strain, count):
    return pl.pallas_call(
        copy_kernel,
        in_specs=[pl.BlockSpec(memory_space=VMEM)],
        out_specs=pl.BlockSpec(memory_space=VMEM),
        out_shape=jax.ShapeDtypeStruct((count, strain.size), jnp.float32),
        compiler_params=pltpu.CompilerParams(vmem_limit_bytes=LIMIT),
    )(strain)


def per_device(strain, basis, recon, nsplit, nshard):
    own = basis[0]
    each = own.shape[0]
    count = nsplit * nshard
    me = lax.axis_index("shard")

    copies = strain_copies(strain, count)
    parts = lax.all_to_all(copies, ("split", "shard"), 0, 0, tiled=True)

    def swap(block, away):
        pairs = [(i, i ^ away) for i in range(nshard)]
        return lax.ppermute(block, "shard", pairs)

    got = {0: own, 4: swap(own, 4), 2: swap(own, 2)}
    got[6] = swap(got[2], 4)
    later, _ = lax.optimization_barrier((own, got[4]))
    got[1], got[3] = swap(later, 1), swap(later, 3)
    got[5], got[7] = swap(got[4], 1), swap(got[4], 3)
    far = [0, 4, 2, 6, 1, 3, 5, 7]
    blocks = [got[away] for away in far]

    nbasis = each * nshard
    depth = -(-nbasis // 256) * 256
    col = lax.broadcasted_iota(jnp.int32, (nbasis, depth), 1)
    row = lax.broadcasted_iota(jnp.int32, (nbasis, depth), 0)
    away = jnp.zeros((nbasis, depth), jnp.int32)
    for place, distance in enumerate(far):
        away = jnp.where(col // each == place, distance, away)
    source = (away ^ me) * each + col % each
    order = ((row == source) & (col < nbasis)).astype(jnp.bfloat16)
    weights = jnp.einsum("qml,lp->qmp", recon[0], order, preferred_element_type=jnp.float32)
    weights = weights.astype(jnp.bfloat16).reshape(-1, depth)

    early, slab = early_series(parts, blocks[:EARLY], strain.shape[0])
    snr, peak = bank(slab, early, blocks[EARLY:], weights)

    peak = jnp.max(spread(peak.reshape(-1), "split", nsplit), axis=0)
    loudest = jnp.max(spread(peak, "shard", nshard), axis=0)
    return (snr[None], loudest)


def solution(mesh):
    body = functools.partial(
        per_device, nsplit=mesh.shape["split"], nshard=mesh.shape["shard"]
    )
    return jax.shard_map(
        body,
        mesh=mesh,
        in_specs=(
            P(None, ("split", "shard")),
            P("split", "shard", None),
            P("split", None, "shard", None),
        ),
        out_specs=(P("split", "shard", None), P()),
        check_vma=False,
    )
```

```python
import functools

import jax
import jax.numpy as jnp
from jax import lax
from jax.experimental import pallas as pl
from jax.experimental.pallas import tpu as pltpu
from jax.sharding import PartitionSpec as P

VMEM = pltpu.VMEM
LIMIT = 30 << 20
COLS = 512
EARLY = 3


def spread(block, axes, count):
    copies = jnp.broadcast_to(block[None], (count,) + block.shape)
    return lax.all_to_all(copies, axes, 0, 0, tiled=True)


def join_strain(parts_ref, lines_ref, turned_ref):
    ndet = lines_ref.shape[0]
    count, piece = parts_ref.shape[0], parts_ref.shape[1] // ndet
    side = 128 // piece
    rows = count // side
    for det in range(ndet):
        cut = slice(det * piece, (det + 1) * piece)
        quarters = [parts_ref[pl.ds(j, rows, stride=side), :][:, cut] for j in range(side)]
        turned_ref[...] = jnp.concatenate(quarters, axis=1)
        for row in range(rows):
            lines_ref[det : det + 1, 128 * row : 128 * row + 128] = turned_ref[row : row + 1, :]


def fill_slab(line, slab_ref, det):
    samples = line.shape[1]
    rows, cols = slab_ref.shape[1:]
    base = jnp.broadcast_to(line, (8, samples))
    first = pltpu.roll(base, samples - 7, 1, stride=1, stride_axis=0)
    turned = [first] + [pltpu.roll(first, samples - 8 * m, 1) for m in range(1, 16)]
    for m in range(1, 16, 2):
        pair = jnp.concatenate([turned[m], turned[m - 1]], axis=0).astype(jnp.bfloat16)
        for q in range(rows // 128):
            row = 16 * ((rows // 8 - 1 - 16 * q - m) // 2)
            slab_ref[det, row : row + 16, :] = pair[:, 128 * q : 128 * q + cols]


def stack_blocks(block_refs, basis_ref):
    row = 0
    for block_ref in block_refs:
        each = block_ref.shape[0]
        basis_ref[row : row + each, :] = block_ref[...]
        row += each


def filtered(basis_ref, slab_ref, det, step, steps):
    taps, cols = basis_ref.shape[1], slab_ref.shape[2]
    start = pl.multiple_of((steps - 1 - step) * cols, cols)
    frame = slab_ref[det, pl.ds(start, taps), :]
    return jnp.dot(basis_ref[...], frame, preferred_element_type=jnp.float32).astype(jnp.bfloat16)


def early_kernel(parts_ref, *refs, blocks):
    block_refs = refs[:blocks]
    out_ref, slab_ref, lines_ref, basis_ref, turned_ref = refs[blocks:]
    ndet, rows, cols = slab_ref.shape
    taps = basis_ref.shape[1]
    join_strain(parts_ref, lines_ref, turned_ref)
    stack_blocks(block_refs, basis_ref)
    for det in range(ndet):
        fill_slab(lines_ref[det : det + 1, :], slab_ref, det)
    for tile in range(out_ref.shape[2] // cols):
        start = rows - taps - tile * cols
        for det in range(ndet):
            frame = slab_ref[det, start : start + taps, :]
            series = jnp.dot(basis_ref[...], frame, preferred_element_type=jnp.float32)
            out_ref[det, :, tile * cols : (tile + 1) * cols] = series.astype(jnp.bfloat16)


def late_kernel(slab_ref, early_ref, weights_ref, *refs, blocks):
    block_refs = refs[:blocks]
    snr_ref, peak_ref, basis_ref, series_ref = refs[blocks:]
    step, steps = pl.program_id(0), pl.num_programs(0)
    ndet, nearly = early_ref.shape[:2]
    nlate = basis_ref.shape[0]

    @pl.when(step == 0)
    def _():
        stack_blocks(block_refs, basis_ref)

    templ = weights_ref.shape[0] // 2

    def fill(det):
        series_ref[det, :nearly, :] = early_ref[det]
        late = filtered(basis_ref, slab_ref, det, step, steps)
        series_ref[det, nearly : nearly + nlate, :] = late

    nbasis = nearly + nlate
    total = None
    fill(0)
    for det in range(ndet):
        if det + 1 < ndet:
            fill(det + 1)
        for quad in range(2):
            rows = weights_ref[quad * templ : (quad + 1) * templ, :nbasis]
            zvals = jnp.dot(rows, series_ref[det], preferred_element_type=jnp.float32)
            total = zvals * zvals if total is None else total + zvals * zvals
    snr = total * (1.0 / (2.0 * ndet))
    snr_ref[...] = snr
    peak_ref[...] = jnp.max(snr, axis=0, keepdims=True)


def early_series(parts, blocks, ndet):
    samples = parts.size // ndet
    taps = blocks[0].shape[1]
    tout = samples - taps
    nearly = sum(block.shape[0] for block in blocks)
    return pl.pallas_call(
        functools.partial(early_kernel, blocks=len(blocks)),
        in_specs=[pl.BlockSpec(memory_space=VMEM)] * (len(blocks) + 1),
        out_specs=[
            pl.BlockSpec(memory_space=VMEM),
            pl.BlockSpec(memory_space=VMEM),
        ],
        out_shape=[
            jax.ShapeDtypeStruct((ndet, nearly, tout), jnp.bfloat16),
            jax.ShapeDtypeStruct((ndet, samples - COLS, COLS), jnp.bfloat16),
        ],
        scratch_shapes=[
            VMEM((ndet, samples), jnp.float32),
            VMEM((nearly, taps), jnp.bfloat16),
            VMEM((samples // 128, 128), jnp.float32),
        ],
        compiler_params=pltpu.CompilerParams(vmem_limit_bytes=LIMIT),
    )(parts, *blocks)


def bank(slab, early, blocks, weights):
    ndet, nearly, tout = early.shape
    taps = blocks[0].shape[1]
    nlate = sum(block.shape[0] for block in blocks)
    templ = weights.shape[0] // 2
    steps = tout // COLS
    whole = pl.BlockSpec(memory_space=VMEM)
    return pl.pallas_call(
        functools.partial(late_kernel, blocks=len(blocks)),
        grid=(steps,),
        in_specs=[whole, pl.BlockSpec((ndet, nearly, COLS), lambda i: (0, 0, i)), whole]
        + [whole] * len(blocks),
        out_specs=[
            pl.BlockSpec((templ, COLS), lambda i: (0, i)),
            pl.BlockSpec((1, COLS), lambda i: (0, i)),
        ],
        out_shape=[
            jax.ShapeDtypeStruct((templ, tout), jnp.float32),
            jax.ShapeDtypeStruct((1, tout), jnp.float32),
        ],
        scratch_shapes=[
            VMEM((nlate, taps), jnp.bfloat16),
            VMEM((ndet, nearly + nlate, COLS), jnp.bfloat16),
        ],
        compiler_params=pltpu.CompilerParams(vmem_limit_bytes=LIMIT),
    )(slab, early, weights, *blocks)


def copy_kernel(strain_ref, copies_ref):
    ndet, piece = strain_ref.shape
    for det in range(ndet):
        row = strain_ref[det : det + 1, :].astype(jnp.float32)
        copies_ref[:, det * piece : (det + 1) * piece] = jnp.broadcast_to(
            row, (copies_ref.shape[0], piece)
        )


def strain_copies(strain, count):
    return pl.pallas_call(
        copy_kernel,
        in_specs=[pl.BlockSpec(memory_space=VMEM)],
        out_specs=pl.BlockSpec(memory_space=VMEM),
        out_shape=jax.ShapeDtypeStruct((count, strain.size), jnp.float32),
        compiler_params=pltpu.CompilerParams(vmem_limit_bytes=LIMIT),
    )(strain)


def per_device(strain, basis, recon, nsplit, nshard):
    own = basis[0]
    each = own.shape[0]
    count = nsplit * nshard
    me = lax.axis_index("shard")

    copies = strain_copies(strain, count)
    parts = lax.all_to_all(copies, ("split", "shard"), 0, 0, tiled=True)

    def swap(block, away):
        pairs = [(i, i ^ away) for i in range(nshard)]
        return lax.ppermute(block, "shard", pairs)

    got = {0: own, 4: swap(own, 4), 2: swap(own, 2)}
    got[6] = swap(got[2], 4)
    later, _ = lax.optimization_barrier((own, got[4]))
    got[1], got[3] = swap(later, 1), swap(later, 3)
    got[5], got[7] = swap(got[4], 1), swap(got[4], 3)
    far = [0, 4, 2, 6, 1, 3, 5, 7]
    blocks = [got[away] for away in far]

    nbasis = each * nshard
    depth = -(-nbasis // 256) * 256
    col = lax.broadcasted_iota(jnp.int32, (nbasis, depth), 1)
    row = lax.broadcasted_iota(jnp.int32, (nbasis, depth), 0)
    away = jnp.zeros((nbasis, depth), jnp.int32)
    for place, distance in enumerate(far):
        away = jnp.where(col // each == place, distance, away)
    source = (away ^ me) * each + col % each
    order = ((row == source) & (col < nbasis)).astype(jnp.bfloat16)
    weights = jnp.einsum("qml,lp->qmp", recon[0], order, preferred_element_type=jnp.float32)
    weights = weights.astype(jnp.bfloat16).reshape(-1, depth)

    early, slab = early_series(parts, blocks[:EARLY], strain.shape[0])
    snr, peak = bank(slab, early, blocks[EARLY:], weights)

    peak = jnp.max(spread(peak.reshape(-1), "split", nsplit), axis=0)
    loudest = jnp.max(spread(peak, "shard", nshard), axis=0)
    return (snr[None], loudest)


def solution(mesh):
    body = functools.partial(
        per_device, nsplit=mesh.shape["split"], nshard=mesh.shape["shard"]
    )
    return jax.shard_map(
        body,
        mesh=mesh,
        in_specs=(
            P(None, ("split", "shard")),
            P("split", "shard", None),
            P("split", None, "shard", None),
        ),
        out_specs=(P("split", "shard", None), P()),
        check_vma=False,
    )
```
